32 devices in a mesh: groups: 2 (over y), seq: 16 (over z, x, core).
Axes of the slice: x: 2, y: 2, z: 4, core: 2. Of those that a mesh axis runs over, the one named last changes fastest.
Arguments:
- queries: bfloat16 [4096, 1536], P(('groups', 'seq')), parts along dimension 0, may hold values from -6 to 6
- keys: bfloat16 [4096, 1536], P(('groups', 'seq')), parts along dimension 0, may hold values from -6 to 6
- values: bfloat16 [4096, 1536], P(('groups', 'seq')), parts along dimension 0, may hold values from -6 to 6
- w_out: bfloat16 [1536, 3072], replicated, may hold values from -0.15625 to 0.15625
- shift_mod: float32 [6144], P('groups'), parts along dimension 0, may hold values from -5 to 5
- scale_mod: float32 [6144], P('groups'), parts along dimension 0, may hold values from -3 to 3
- w_final: bfloat16 [3072, 64], replicated, may hold values from -0.109375 to 0.109375
- conv_weight: bfloat16 [432, 512], replicated, may hold values from -0.3125 to 0.3125
- conv_bias: float32 [512], replicated, may hold values from -3 to 3
Outputs:
- decoded: bfloat16 [8, 32, 64, 512], P('groups', 'seq'), parts along dimension 0
The draws below stay inside these ranges and needn't reach their ends.
There are 2 independent parts, one for each index of `groups`. The reference program is written for one: setup_inputs(seed, part) draws one part's arguments, and reference() takes and returns one part's arrays. A program takes and returns all parts, laid end to end along the dimension named above; an argument that names none is the same for every part. Nothing has to cross between parts.
All inputs are finite; a program needn't handle non-finite values.
Results may differ from the reference program's by a relative error of at most 0.018.
Values may be sent and summed in bfloat16 or wider, within the bound.
A program may use at most 192 MiB of HBM per device.

```python
import math
import jax
import jax.numpy as jnp
from jax import lax

D = 3072
HEADS = 12
HEAD_DIM = 128
LATENT_CH = 16
CONV_CH = 512
FRAMES = 4
ROWS = 32
TOKENS = 2048


def draw_queries(key, part):
    base = jnp.clip(jax.random.normal(jax.random.fold_in(key, 1), (TOKENS, HEADS * HEAD_DIM), jnp.float32), -6.0, 6.0)
    return base.astype(jnp.bfloat16)


def draw_keys(key, part):
    base = jnp.clip(jax.random.normal(jax.random.fold_in(key, 2), (TOKENS, HEADS * HEAD_DIM), jnp.float32), -6.0, 6.0)
    return base.astype(jnp.bfloat16)


def shard_levels(stream_key, dims, shards, smallest, high):
    factor_of, own = 1.0, jax.random.fold_in(stream_key, 6)
    for dim, blocks in shards:
        steps = jnp.exp(jax.random.uniform(jax.random.fold_in(own, dim), (blocks,), jnp.float32, smallest / len(shards), high / len(shards)))
        factor_of = factor_of * jnp.repeat(steps, dims[dim] // blocks).reshape([-1 if axis == dim else 1 for axis in range(len(dims))])
    return factor_of


def scatter_about(own_key, extent, scale, most, cuts=(), kind=jnp.bfloat16):
    drawn = scale * jax.random.normal(own_key, extent, jnp.float32)
    if cuts:
        drawn = drawn * shard_levels(own_key, extent, cuts, -0.22, 0.18)
    return jnp.clip(drawn, -most, most).astype(kind)


def setup_inputs(seed: int = 0, part: int = 0) -> dict:
    key_of = jax.random.split(jax.random.key(seed), 10)
    part_splits = jax.random.split(jax.random.fold_in(key_of[9], part), 10)
    queries = draw_queries(jax.random.fold_in(jax.random.fold_in(key_of[9], part), 71), part)
    keys = draw_keys(jax.random.fold_in(jax.random.fold_in(key_of[9], part), 71), part)
    values = scatter_about(part_splits[2], (TOKENS, HEADS * HEAD_DIM), 1.0, 6.0, ((0, 16),))
    w_out = scatter_about(key_of[3], (HEADS * HEAD_DIM, D), (HEADS * HEAD_DIM) ** -0.5, 0.15625)
    shift_mod = scatter_about(part_splits[4], (D,), 1.0, 5.0, (), jnp.float32)
    scale_mod = scatter_about(part_splits[5], (D,), 0.5, 3.0, (), jnp.float32)
    w_final = scatter_about(key_of[6], (D, 4 * LATENT_CH), D ** -0.5, 0.109375)
    conv_weight = scatter_about(key_of[7], (27 * LATENT_CH, CONV_CH), (27 * LATENT_CH) ** -0.5, 0.3125)
    conv_bias = scatter_about(key_of[8], (CONV_CH,), 0.5, 3.0, (), jnp.float32)
    return {"queries": queries, "keys": keys, "values": values, "w_out": w_out, "shift_mod": shift_mod, "scale_mod": scale_mod, "w_final": w_final, "conv_weight": conv_weight, "conv_bias": conv_bias}


def convolve(padded, conv_weight, conv_bias, frames, width, height):
    taps = []
    for shift_t in range(3):
        for shift_x in range(3):
            for shift_y in range(3):
                taps.append(padded[shift_t:shift_t + frames, shift_x:shift_x + width, shift_y:shift_y + height, :])
    stacked = jnp.concatenate(taps, axis=3)
    flat = stacked.reshape(frames * width * height, stacked.shape[3])
    output = jnp.dot(flat, conv_weight, preferred_element_type=jnp.float32) + conv_bias
    return output.astype(jnp.bfloat16).reshape(frames, width, height, conv_weight.shape[1])

def reference(queries, keys, values, w_out, shift_mod, scale_mod, w_final, conv_weight, conv_bias):
    tokens = queries.shape[0]
    inv_root = 1.0 / math.sqrt(HEAD_DIM)
    query_heads = queries.astype(jnp.float32).reshape(tokens, HEADS, HEAD_DIM).transpose(1, 0, 2)
    key_heads = keys.astype(jnp.float32).reshape(tokens, HEADS, HEAD_DIM).transpose(1, 0, 2)
    value_heads = values.reshape(tokens, HEADS, HEAD_DIM).transpose(1, 0, 2)
    block_rows = min(2048, tokens)

    def per_head(operands):
        query_h, key_h, value_h = operands

        def per_block(query_b):
            scores = jnp.dot(query_b, key_h.T, precision=lax.Precision.HIGHEST) * inv_root
            peak = lax.optimization_barrier(jnp.max(scores, axis=1, keepdims=True))
            exp_scores = jnp.exp(scores - peak)
            weights = lax.optimization_barrier(exp_scores.astype(jnp.bfloat16))
            summed = jnp.dot(weights, value_h, preferred_element_type=jnp.float32)
            return (summed / lax.optimization_barrier(jnp.sum(exp_scores, axis=1, keepdims=True))).astype(jnp.bfloat16)
        query_blocks = query_h.reshape(tokens // block_rows, block_rows, HEAD_DIM)
        return lax.map(per_block, query_blocks).reshape(tokens, HEAD_DIM)
    attended = lax.map(per_head, (query_heads, key_heads, value_heads))
    attended = attended.transpose(1, 0, 2).reshape(tokens, HEADS * HEAD_DIM)
    projected = jnp.dot(attended, w_out, preferred_element_type=jnp.float32)
    centered = projected - lax.optimization_barrier(jnp.mean(projected, axis=1, keepdims=True))
    variance = lax.optimization_barrier(jnp.mean(centered * centered, axis=1, keepdims=True))
    normed = (centered * lax.rsqrt(variance + 1e-06) * (1.0 + scale_mod) + shift_mod).astype(jnp.bfloat16)
    patches = jnp.dot(normed, w_final, preferred_element_type=jnp.float32).astype(jnp.bfloat16)
    columns = tokens // (FRAMES * ROWS)
    latent = patches.reshape(FRAMES, ROWS, columns, LATENT_CH, 2, 2).transpose(0, 2, 5, 1, 4, 3)
    latent = latent.reshape(FRAMES, 2 * columns, 2 * ROWS, LATENT_CH)
    padded = jnp.pad(latent, ((2, 0), (1, 1), (1, 1), (0, 0)), mode='edge')
    return convolve(padded, conv_weight, conv_bias, FRAMES, 2 * columns, 2 * ROWS)
```

```python
import functools
import math

import jax
import jax.numpy as jnp
from jax import lax
from jax.experimental import pallas as pl
from jax.experimental.pallas import tpu as pltpu
from jax.sharding import PartitionSpec as P

HEADS = 12
HEAD_DIM = 128
HEAD_GROUPS = 4
LATENT_CH = 16
FRAMES = 4
ROWS = 32
PER_HEAD = HEADS // HEAD_GROUPS
WIDTH = PER_HEAD * HEAD_DIM
BF = jnp.bfloat16
F32 = jnp.float32


def mm(a, b):
    return lax.dot_general(a, b, (((1,), (0,)), ((), ())), preferred_element_type=F32)


def iota(shape, dim):
    return lax.broadcasted_iota(jnp.int32, shape, dim)


def ones_where(cond):
    return jnp.where(cond, 1.0, 0.0).astype(BF)


def kernel(
    n,
    q_ref, k_ref, v_ref, w_out_hbm, shift_ref, scale_ref, w_final_hbm, conv_w_hbm, bias_ref,
    out_ref,
    qb, kb, vb, m_ref, l_ref, acc_ref, ob, att, w_out_v, w_final_v, conv_v, big_w, proj, send_b, recv_b,
    z_send, z_recv, g_send, g_recv, o_send, o_recv, e_send, e_recv, loc,
):
    me = lax.axis_index("seq")
    blk = n // HEAD_GROUPS
    grp = me // blk
    pos = me % blk
    tok = q_ref.shape[0]
    rows_dev = tok // n
    bits = [1 << i for i in reversed(range(blk.bit_length() - 1))]

    def cols(g):
        return pl.ds(pl.multiple_of(g * WIDTH, 128), WIDTH)

    def remote(src, dst, ssem, rsem, dev):
        return pltpu.make_async_remote_copy(
            src_ref=src, dst_ref=dst, send_sem=ssem, recv_sem=rsem,
            device_id={"seq": dev}, device_id_type=pl.DeviceIdType.MESH,
        )

    barrier = pltpu.get_barrier_semaphore()

    def greet(i, c):
        pl.semaphore_signal(
            barrier, inc=1, device_id={"seq": (me + i) % n}, device_id_type=pl.DeviceIdType.MESH
        )
        return c

    lax.fori_loop(1, n, greet, 0)

    srcs = (q_ref, k_ref, v_ref)
    own = [
        pltpu.make_async_copy(q_ref.at[:, cols(grp)], qb.at[grp], loc.at[0]),
        pltpu.make_async_copy(k_ref.at[:, cols(grp)], kb.at[grp, pos], loc.at[1]),
        pltpu.make_async_copy(v_ref.at[:, cols(grp)], vb.at[grp, pos], loc.at[2]),
    ]
    weights = [
        pltpu.make_async_copy(w_out_hbm, w_out_v, loc.at[3]),
        pltpu.make_async_copy(w_final_hbm, w_final_v, loc.at[4]),
        pltpu.make_async_copy(conv_w_hbm, conv_v, loc.at[5]),
    ]
    for c in own + weights[::-1]:
        c.start()
    pl.semaphore_wait(barrier, n - 1)

    def z_copy(t, j):
        tgt = (grp + j) % HEAD_GROUPS
        dst = (qb.at[grp], kb.at[grp, pos], vb.at[grp, pos])[t]
        return remote(srcs[t].at[:, cols(tgt)], dst, z_send.at[t, j], z_recv.at[t, j], tgt * blk + pos)

    def z_wait(t, j):
        src = (grp + HEAD_GROUPS - j) % HEAD_GROUPS
        dst = (qb.at[src], kb.at[src, pos], vb.at[src, pos])[t]
        remote(dst, dst, z_send.at[t, j], z_recv.at[t, j], src * blk + pos).wait_recv()

    bufs = (None, kb, vb)

    def g_copy(t, j, mask, bit):
        slot = (grp + HEAD_GROUPS - j) % HEAD_GROUPS
        if j == 0 and mask == 0:
            src = srcs[t].at[:, cols(grp)]
        else:
            src = bufs[t].at[slot, pos ^ mask]
        return remote(
            src, bufs[t].at[slot, pos ^ mask],
            g_send.at[t - 1, j, mask | bit], g_recv.at[t - 1, j, mask | bit], grp * blk + (pos ^ bit),
        )

    def g_wait(t, j, mask):
        slot = (grp + HEAD_GROUPS - j) % HEAD_GROUPS
        dst = bufs[t].at[slot, pos ^ mask]
        bit = mask & -mask
        remote(
            dst, dst, g_send.at[t - 1, j, mask], g_recv.at[t - 1, j, mask], grp * blk + (pos ^ bit)
        ).wait_recv()

    sent = []

    def forward(t, j, mask):
        for bit in bits:
            if mask == 0 or bit < (mask & -mask):
                c = g_copy(t, j, mask, bit)
                c.start()
                sent.append(c)

    inner = sorted(range(1, blk), key=lambda m: -(m & -m))

    def gather_rest(j):
        for mask in inner:
            for t in (1, 2):
                g_wait(t, j, mask)
                forward(t, j, mask)

    for j in range(1, HEAD_GROUPS):
        c = z_copy(0, j)
        c.start()
        sent.append(c)
    for t in (1, 2):
        forward(t, 0, 0)
    for j in range(1, HEAD_GROUPS):
        for t in (1, 2):
            c = z_copy(t, j)
            c.start()
            sent.append(c)

    m_ref[...] = jnp.full(m_ref.shape, -1e30, F32)
    l_ref[...] = jnp.zeros(l_ref.shape, F32)
    acc_ref[...] = jnp.zeros(acc_ref.shape, F32)
    weights[2].wait()
    big_w[...] = jnp.zeros(big_w.shape, BF)
    out_ch = conv_v.shape[1]
    for a in range(3):
        for e in range(3):
            for b in range(3):
                for s in range(2):
                    big_w[
                        (a * 3 + e) * 64 + (b + s) * 16 : (a * 3 + e) * 64 + (b + s) * 16 + 16,
                        s * out_ch : (s + 1) * out_ch,
                    ] = conv_v[(9 * a + 3 * b + e) * 16 : (9 * a + 3 * b + e) * 16 + 16, :]

    for c in own:
        c.wait()
    gather_rest(0)
    for j in range(1, HEAD_GROUPS):
        z_wait(0, j)

    queries = HEAD_GROUPS * tok
    part = min(blk, 4)
    factor = math.log2(math.e) / math.sqrt(HEAD_DIM)

    def attend(slot):
        def some(i, c):
            for h in range(PER_HEAD):
                hs = slice(h * HEAD_DIM, (h + 1) * HEAD_DIM)
                qh = qb[:, :, hs].reshape(queries, HEAD_DIM)
                kh = kb[slot, pl.ds(i * part, part), :, hs].reshape(part * tok, HEAD_DIM)
                vh = vb[slot, pl.ds(i * part, part), :, hs].reshape(part * tok, HEAD_DIM)
                s = lax.dot_general(qh, kh, (((1,), (1,)), ((), ())), preferred_element_type=F32)
                s = s * factor
                old = m_ref[h]
                new = jnp.maximum(old, jnp.max(s, axis=1, keepdims=True))
                p = jnp.exp2(s - new)
                alpha = jnp.exp2(old - new)
                l_ref[h] = l_ref[h] * alpha + jnp.sum(p, axis=1, keepdims=True)
                acc_ref[h] = acc_ref[h] * alpha + mm(p.astype(BF), vh)
                m_ref[h] = new
            return c

        lax.fori_loop(0, blk // part, some, 0)

    attend(grp)
    for j in range(1, HEAD_GROUPS):
        for t in (1, 2):
            z_wait(t, j)
            forward(t, j, 0)
        gather_rest(j)
        attend((grp + HEAD_GROUPS - j) % HEAD_GROUPS)

    for h in range(PER_HEAD):
        res = (acc_ref[h] / l_ref[h]).astype(BF)
        ob[:, :, h * HEAD_DIM : (h + 1) * HEAD_DIM] = res.reshape(HEAD_GROUPS, tok, HEAD_DIM)
    for j in range(1, HEAD_GROUPS):
        tgt = (grp + j) % HEAD_GROUPS
        c = remote(ob.at[tgt], att.at[grp], o_send.at[j], o_recv.at[j], tgt * blk + pos)
        c.start()
        sent.append(c)
    weights[0].wait()
    proj[...] = mm(ob[grp], w_out_v[grp])
    for j in range(1, HEAD_GROUPS):
        src = (grp + HEAD_GROUPS - j) % HEAD_GROUPS
        remote(att.at[src], att.at[src], o_send.at[j], o_recv.at[j], src * blk + pos).wait_recv()
        proj[...] += mm(att[src], w_out_v[src])
    projected = proj[...]
    centered = projected - jnp.mean(projected, axis=1, keepdims=True)
    variance = jnp.mean(centered * centered, axis=1, keepdims=True)
    normed = (
        centered * lax.rsqrt(variance + 1e-06) * (1.0 + scale_ref[...]) + shift_ref[...]
    ).astype(BF)
    weights[1].wait()
    patches = mm(normed, w_final_v[...]).astype(BF)

    ch = iota((4 * LATENT_CH, 128), 0)
    lane = iota((4 * LATENT_CH, 128), 1)
    base = 4 * (lane % 16) + 2 * (lane // 64)
    xcol = (lane // 16) % 4
    row = iota((tok, tok), 0)
    col = iota((tok, tok), 1)
    w = row // rows_dev
    here = (row % rows_dev) * n + w
    picks = (
        ((col == here - 1) & (w > 0), (xcol == 0) & (ch == base + 1)),
        ((col == here) & (w == 0), (xcol == 0) & (ch == base)),
        (col == here, ((xcol == 1) & (ch == base)) | ((xcol == 2) & (ch == base + 1))),
        ((col == here + 1) & (w < n - 1), (xcol == 3) & (ch == base)),
        ((col == here) & (w == n - 1), (xcol == 3) & (ch == base + 1)),
    )
    window = None
    for rows_pick, ch_pick in picks:
        term = mm(ones_where(rows_pick), mm(patches, ones_where(ch_pick)).astype(BF))
        window = term if window is None else window + term
    send_b[...] = window.reshape(n, rows_dev, 128)

    def e_copy(i):
        dev = (me + i) % n
        return remote(send_b.at[dev], recv_b.at[me], e_send.at[i], e_recv.at[i], dev)

    def e_start(i, c):
        e_copy(i).start()
        return c

    def e_wait(i, c):
        src = (me + n - i) % n
        remote(recv_b.at[src], recv_b.at[src], e_send.at[i], e_recv.at[i], src).wait_recv()
        e_copy(i).wait_send()
        return c

    lax.fori_loop(1, n, e_start, 0)
    recv_b[me] = send_b[me]
    lax.fori_loop(1, n, e_wait, 0)
    for c in sent:
        c.wait_send()

    got = recv_b[...].reshape(FRAMES * ROWS, 128)
    turned = pltpu.roll(got, 64, 1)
    low = iota(got.shape, 1) < 64
    lo = jnp.concatenate([jnp.where(low, got, 0.0), jnp.where(low, turned, 0.0)], axis=0).astype(BF)
    hi = jnp.concatenate([jnp.where(low, 0.0, turned), jnp.where(low, 0.0, got)], axis=0).astype(BF)
    cells = FRAMES * 2 * ROWS
    orow = iota((cells, cells), 0)
    ocol = iota((cells, cells), 1)
    of = orow // (2 * ROWS)
    oy = orow % (2 * ROWS)

    def pick(idx):
        a, e = idx // 3, idx % 3
        sf = jnp.maximum(of + (a - 2), 0)
        sy = jnp.clip(oy + (e - 1), 0, 2 * ROWS - 1)
        return ones_where(ocol == (sy % 2) * (FRAMES * ROWS) + sf * ROWS + sy // 2)

    feats = []
    for pair in range(5):
        x = mm(pick(2 * pair), lo)
        if 2 * pair + 1 < 9:
            x = x + mm(pick(2 * pair + 1), hi)
        feats.append(x.astype(BF))
    feats = jnp.concatenate(feats, axis=1)
    for s in range(2):
        res = mm(feats, big_w[:, s * out_ch : (s + 1) * out_ch]) + bias_ref[...]
        res = res.astype(BF)
        for f in range(FRAMES):
            out_ref[f, s] = res[f * 2 * ROWS : (f + 1) * 2 * ROWS]


def shards(queries, keys, values, w_out, shift_mod, scale_mod, w_final, conv_weight, conv_bias):
    n = lax.axis_size("seq")
    blk = n // HEAD_GROUPS
    tok = queries.shape[0]
    d = w_out.shape[1]
    out_ch = conv_weight.shape[1]
    vm = pl.BlockSpec(memory_space=pltpu.VMEM)
    hbm = pl.BlockSpec(memory_space=pl.ANY)
    dma = pltpu.SemaphoreType.DMA
    qn = HEAD_GROUPS * tok
    return pl.pallas_call(
        functools.partial(kernel, n),
        out_shape=jax.ShapeDtypeStruct((FRAMES, 2, 2 * ROWS, out_ch), BF),
        in_specs=[vm, vm, vm, hbm, vm, vm, hbm, hbm, vm],
        out_specs=vm,
        scratch_shapes=[
            pltpu.VMEM((HEAD_GROUPS, tok, WIDTH), BF),
            pltpu.VMEM((HEAD_GROUPS, blk, tok, WIDTH), BF),
            pltpu.VMEM((HEAD_GROUPS, blk, tok, WIDTH), BF),
            pltpu.VMEM((PER_HEAD, qn, 1), F32),
            pltpu.VMEM((PER_HEAD, qn, 1), F32),
            pltpu.VMEM((PER_HEAD, qn, HEAD_DIM), F32),
            pltpu.VMEM((HEAD_GROUPS, tok, WIDTH), BF),
            pltpu.VMEM((HEAD_GROUPS, tok, WIDTH), BF),
            pltpu.VMEM((HEAD_GROUPS, WIDTH, d), BF),
            pltpu.VMEM(w_final.shape, BF),
            pltpu.VMEM(conv_weight.shape, BF),
            pltpu.VMEM((640, 2 * out_ch), BF),
            pltpu.VMEM((tok, d), F32),
            pltpu.VMEM((n, tok // n, 128), F32),
            pltpu.VMEM((n, tok // n, 128), F32),
            dma((3, HEAD_GROUPS)), dma((3, HEAD_GROUPS)),
            dma((2, HEAD_GROUPS, blk)), dma((2, HEAD_GROUPS, blk)),
            dma((HEAD_GROUPS,)), dma((HEAD_GROUPS,)),
            dma((n,)), dma((n,)),
            dma((6,)),
        ],
        compiler_params=pltpu.CompilerParams(
            collective_id=0, has_side_effects=True, vmem_limit_bytes=60 * 1024 * 1024
        ),
        name="fused",
    )(
        queries, keys, values, w_out.reshape(HEAD_GROUPS, WIDTH, d),
        shift_mod.reshape(1, d), scale_mod.reshape(1, d), w_final, conv_weight,
        conv_bias.reshape(1, out_ch),
    )


def solution(mesh):
    placed = (
        P(("groups", "seq"), None),
        P(("groups", "seq"), None),
        P(("groups", "seq"), None),
        P(),
        P("groups"),
        P("groups"),
        P(),
        P(),
        P(),
    )
    return jax.shard_map(
        shards,
        mesh=mesh,
        in_specs=placed,
        out_specs=P("groups", "seq", None, None),
        check_vma=False,
    )
```

```python
import functools
import math

import jax
import jax.numpy as jnp
from jax import lax
from jax.experimental import pallas as pl
from jax.experimental.pallas import tpu as pltpu
from jax.sharding import PartitionSpec as P

HEADS = 12
HEAD_DIM = 128
HEAD_GROUPS = 4
LATENT_CH = 16
FRAMES = 4
ROWS = 32
PER_HEAD = HEADS // HEAD_GROUPS
WIDTH = PER_HEAD * HEAD_DIM
BF = jnp.bfloat16
F32 = jnp.float32


def mm(a, b):
    return lax.dot_general(a, b, (((1,), (0,)), ((), ())), preferred_element_type=F32)


def iota(shape, dim):
    return lax.broadcasted_iota(jnp.int32, shape, dim)


def ones_where(cond):
    return jnp.where(cond, 1.0, 0.0).astype(BF)


def kernel(
    n,
    q_ref, k_ref, v_ref, w_out_hbm, shift_ref, scale_ref, w_final_hbm,
    out_ref,
    qb, kb, vb, m_ref, l_ref, acc_ref, ob, att, w_out_v, w_final_v, proj, send_b, recv_b,
    z_send, z_recv, g_send, g_recv, o_send, o_recv, e_send, e_recv, loc,
):
    me = lax.axis_index("seq")
    blk = n // HEAD_GROUPS
    grp = me // blk
    pos = me % blk
    tok = q_ref.shape[0]
    rows_dev = tok // n
    bits = [1 << i for i in reversed(range(blk.bit_length() - 1))]

    def cols(g, h):
        return pl.ds(pl.multiple_of(g * WIDTH + h * HEAD_DIM, 128), HEAD_DIM)

    def remote(src, dst, ssem, rsem, dev):
        return pltpu.make_async_remote_copy(
            src_ref=src, dst_ref=dst, send_sem=ssem, recv_sem=rsem,
            device_id={"seq": dev}, device_id_type=pl.DeviceIdType.MESH,
        )

    barrier = pltpu.get_barrier_semaphore()

    def greet(i, c):
        pl.semaphore_signal(
            barrier, inc=1, device_id={"seq": (me + i) % n}, device_id_type=pl.DeviceIdType.MESH
        )
        return c

    lax.fori_loop(1, n, greet, 0)

    srcs = (q_ref, k_ref, v_ref)
    bufs = (qb, kb, vb)

    def home(t, h, slot):
        return qb.at[h, slot] if t == 0 else bufs[t].at[h, slot, pos]

    own = [
        pltpu.make_async_copy(srcs[t].at[:, cols(grp, h)], home(t, h, grp), loc.at[h * 3 + t])
        for h in range(PER_HEAD)
        for t in range(3)
    ]
    w_out_copies = [
        pltpu.make_async_copy(w_out_hbm.at[:, h], w_out_v.at[h], loc.at[9 + h]) for h in range(PER_HEAD)
    ]
    w_final_copy = pltpu.make_async_copy(w_final_hbm, w_final_v, loc.at[12])
    for c in own + w_out_copies + [w_final_copy]:
        c.start()
    pl.semaphore_wait(barrier, n - 1)

    def slot_of(j):
        return (grp + HEAD_GROUPS - j) % HEAD_GROUPS

    sent = []

    def z_start(t, h, j):
        tgt = (grp + j) % HEAD_GROUPS
        c = remote(
            srcs[t].at[:, cols(tgt, h)], home(t, h, grp),
            z_send.at[t, h, j], z_recv.at[t, h, j], tgt * blk + pos,
        )
        c.start()
        sent.append(c)

    def z_wait(t, h, j):
        dst = home(t, h, slot_of(j))
        remote(dst, dst, z_send.at[t, h, j], z_recv.at[t, h, j], slot_of(j) * blk + pos).wait_recv()

    def g_copy(t, h, j, mask, bit, src=None):
        dst = bufs[t].at[h, slot_of(j), pos ^ mask]
        return remote(
            dst if src is None else src, dst,
            g_send.at[t - 1, h, j, mask + bit], g_recv.at[t - 1, h, j, mask + bit],
            grp * blk + (pos ^ bit),
        )

    def g_wait(t, h, j, mask, bit):
        dst = bufs[t].at[h, slot_of(j), pos ^ mask]
        remote(
            dst, dst, g_send.at[t - 1, h, j, mask], g_recv.at[t - 1, h, j, mask], grp * blk + (pos ^ bit)
        ).wait_recv()

    def first(h, j):
        for t in (1, 2):
            if j:
                z_wait(t, h, j)
            for bit in bits:
                g_copy(t, h, j, 0, bit, None if j else srcs[t].at[:, cols(grp, h)]).start()

    def relay(h, j, some_bits):
        for bit in some_bits:

            def one(i, c):
                mask = bit + i * (2 * bit)
                for t in (1, 2):
                    g_wait(t, h, j, mask, bit)
                    for low in bits:
                        if low < bit:
                            g_copy(t, h, j, mask, low).start()
                return c

            lax.fori_loop(0, blk // (2 * bit), one, 0)

    for h in range(PER_HEAD):
        for j in range(1, HEAD_GROUPS):
            z_start(0, h, j)
        if h == 0:
            first(0, 0)
        for j in range(1, HEAD_GROUPS):
            for t in (1, 2):
                z_start(t, h, j)

    m_ref[...] = jnp.full(m_ref.shape, -1e30, F32)
    l_ref[...] = jnp.zeros(l_ref.shape, F32)
    acc_ref[...] = jnp.zeros(acc_ref.shape, F32)
    for c in own:
        c.wait()

    queries = HEAD_GROUPS * tok
    part = min(blk, 4)
    factor = math.log2(math.e) / math.sqrt(HEAD_DIM)

    def attend(h, slot):
        def some(i, c):
            qh = qb[h].reshape(queries, HEAD_DIM)
            kh = kb[h, slot, pl.ds(i * part, part)].reshape(part * tok, HEAD_DIM)
            vh = vb[h, slot, pl.ds(i * part, part)].reshape(part * tok, HEAD_DIM)
            s = lax.dot_general(qh, kh, (((1,), (1,)), ((), ())), preferred_element_type=F32)
            s = s * factor
            old = m_ref[h]
            new = jnp.maximum(old, jnp.max(s, axis=1, keepdims=True))
            p = jnp.exp2(s - new)
            alpha = jnp.exp2(old - new)
            l_ref[h] = l_ref[h] * alpha + jnp.sum(p, axis=1, keepdims=True)
            acc_ref[h] = acc_ref[h] * alpha + mm(p.astype(BF), vh)
            m_ref[h] = new
            return c

        lax.fori_loop(0, blk // part, some, 0)

    def finish(h):
        ob[h] = (acc_ref[h] / l_ref[h]).astype(BF).reshape(HEAD_GROUPS, tok, HEAD_DIM)
        lanes = pl.ds(pl.multiple_of(grp * HEAD_DIM, 128), HEAD_DIM)
        for j in range(1, HEAD_GROUPS):
            tgt = (grp + j) % HEAD_GROUPS
            c = remote(
                ob.at[h, tgt], att.at[h, :, lanes], o_send.at[h, j], o_recv.at[h, j], tgt * blk + pos
            )
            c.start()
            sent.append(c)
        att[h, :, lanes] = ob[h, grp]

    units = [(h, j) for h in range(PER_HEAD) for j in range(HEAD_GROUPS)]
    count = len(units)
    for u in range(-2, count):
        if 0 <= u + 2 < count and u + 2 > 0:
            first(*units[u + 2])
        if 0 <= u + 1 < count:
            relay(*units[u + 1], bits[:-1])
        if u >= 0:
            h, j = units[u]
            relay(h, j, bits[-1:])
            if j == 0:
                for i in range(1, HEAD_GROUPS):
                    z_wait(0, h, i)
            attend(h, slot_of(j))
            if j == HEAD_GROUPS - 1:
                finish(h)

    for h in range(PER_HEAD):
        w_out_copies[h].wait()
        for j in range(1, HEAD_GROUPS):
            lanes = pl.ds(pl.multiple_of(slot_of(j) * HEAD_DIM, 128), HEAD_DIM)
            dst = att.at[h, :, lanes]
            remote(dst, dst, o_send.at[h, j], o_recv.at[h, j], slot_of(j) * blk + pos).wait_recv()
        term = mm(att[h], w_out_v[h].reshape(HEAD_GROUPS * HEAD_DIM, proj.shape[1]))
        proj[...] = term if h == 0 else proj[...] + term
    projected = proj[...]
    centered = projected - jnp.mean(projected, axis=1, keepdims=True)
    variance = jnp.mean(centered * centered, axis=1, keepdims=True)
    normed = (
        centered * lax.rsqrt(variance + 1e-06) * (1.0 + scale_ref[...]) + shift_ref[...]
    ).astype(BF)
    w_final_copy.wait()
    patches = lax.dot_general(
        normed, w_final_v[...], (((1,), (1,)), ((), ())), preferred_element_type=F32
    ).astype(BF)

    ch = iota((4 * LATENT_CH, 128), 0)
    lane = iota((4 * LATENT_CH, 128), 1)
    base = 4 * (lane % 16) + 2 * (lane // 64)
    xcol = (lane // 16) % 4
    row = iota((tok, tok), 0)
    col = iota((tok, tok), 1)
    w = row // rows_dev
    here = (row % rows_dev) * n + w
    picks = (
        ((col == here - 1) & (w > 0), (xcol == 0) & (ch == base + 1)),
        ((col == here) & (w == 0), (xcol == 0) & (ch == base)),
        (col == here, ((xcol == 1) & (ch == base)) | ((xcol == 2) & (ch == base + 1))),
        ((col == here + 1) & (w < n - 1), (xcol == 3) & (ch == base)),
        ((col == here) & (w == n - 1), (xcol == 3) & (ch == base + 1)),
    )
    window = None
    for rows_pick, ch_pick in picks:
        term = mm(ones_where(rows_pick), mm(patches, ones_where(ch_pick)).astype(BF))
        window = term if window is None else window + term
    send_b[...] = window.reshape(n, rows_dev, 128)

    def e_copy(i):
        dev = (me + i) % n
        return remote(send_b.at[dev], recv_b.at[me], e_send.at[i], e_recv.at[i], dev)

    def e_start(i, c):
        e_copy(i).start()
        return c

    def e_wait(i, c):
        src = (me + n - i) % n
        remote(recv_b.at[src], recv_b.at[src], e_send.at[i], e_recv.at[i], src).wait_recv()
        e_copy(i).wait_send()
        return c

    lax.fori_loop(1, n, e_start, 0)
    recv_b[me] = send_b[me]
    lax.fori_loop(1, n, e_wait, 0)
    for c in sent:
        c.wait_send()

    def drain(i, c):
        h = i // (HEAD_GROUPS * (blk - 1))
        j = (i // (blk - 1)) % HEAD_GROUPS
        mask = i % (blk - 1) + 1
        for t in (1, 2):
            ref = bufs[t].at[0, 0, 0]
            remote(
                ref, ref, g_send.at[t - 1, h, j, mask], g_recv.at[t - 1, h, j, mask], (me + 1) % n
            ).wait_send()
        return c

    lax.fori_loop(0, PER_HEAD * HEAD_GROUPS * (blk - 1), drain, 0)
    out_ref[...] = recv_b[...].reshape(out_ref.shape)


def conv_kernel(got_ref, conv_v, bias_ref, out_ref, big_w):
    out_ch = conv_v.shape[1]
    big_w[...] = jnp.zeros(big_w.shape, BF)
    for a in range(3):
        for e in range(3):
            for b in range(3):
                for s in range(2):
                    big_w[
                        (a * 3 + e) * 64 + (b + s) * 16 : (a * 3 + e) * 64 + (b + s) * 16 + 16,
                        s * out_ch : (s + 1) * out_ch,
                    ] = conv_v[(9 * a + 3 * b + e) * 16 : (9 * a + 3 * b + e) * 16 + 16, :]
    got = got_ref[...]
    turned = pltpu.roll(got, 64, 1)
    low = iota(got.shape, 1) < 64
    lo = jnp.concatenate([jnp.where(low, got, 0.0), jnp.where(low, turned, 0.0)], axis=0).astype(BF)
    hi = jnp.concatenate([jnp.where(low, 0.0, turned), jnp.where(low, 0.0, got)], axis=0).astype(BF)
    cells = FRAMES * 2 * ROWS
    orow = iota((cells, cells), 0)
    ocol = iota((cells, cells), 1)
    of = orow // (2 * ROWS)
    oy = orow % (2 * ROWS)

    def pick(idx):
        a, e = idx // 3, idx % 3
        sf = jnp.maximum(of + (a - 2), 0)
        sy = jnp.clip(oy + (e - 1), 0, 2 * ROWS - 1)
        return ones_where(ocol == (sy % 2) * (FRAMES * ROWS) + sf * ROWS + sy // 2)

    feats = []
    for pair in range(5):
        x = mm(pick(2 * pair), lo)
        if 2 * pair + 1 < 9:
            x = x + mm(pick(2 * pair + 1), hi)
        feats.append(x.astype(BF))
    feats = jnp.concatenate(feats, axis=1)
    for s in range(2):
        res = mm(feats, big_w[:, s * out_ch : (s + 1) * out_ch]) + bias_ref[...]
        res = res.astype(BF)
        for f in range(FRAMES):
            out_ref[f, s] = res[f * 2 * ROWS : (f + 1) * 2 * ROWS]

def shards(queries, keys, values, w_out, shift_mod, scale_mod, w_final, conv_weight, conv_bias):
    n = lax.axis_size("seq")
    blk = n // HEAD_GROUPS
    tok = queries.shape[0]
    d = w_out.shape[1]
    out_ch = conv_weight.shape[1]
    vm = pl.BlockSpec(memory_space=pltpu.VMEM)
    hbm = pl.BlockSpec(memory_space=pl.ANY)
    dma = pltpu.SemaphoreType.DMA
    qn = HEAD_GROUPS * tok
    got = pl.pallas_call(
        functools.partial(kernel, n),
        out_shape=jax.ShapeDtypeStruct((FRAMES * ROWS, 128), F32),
        in_specs=[vm, vm, vm, hbm, vm, vm, hbm],
        out_specs=vm,
        scratch_shapes=[
            pltpu.VMEM((PER_HEAD, HEAD_GROUPS, tok, HEAD_DIM), BF),
            pltpu.VMEM((PER_HEAD, HEAD_GROUPS, blk, tok, HEAD_DIM), BF),
            pltpu.VMEM((PER_HEAD, HEAD_GROUPS, blk, tok, HEAD_DIM), BF),
            pltpu.VMEM((PER_HEAD, qn, 1), F32),
            pltpu.VMEM((PER_HEAD, qn, 1), F32),
            pltpu.VMEM((PER_HEAD, qn, HEAD_DIM), F32),
            pltpu.VMEM((PER_HEAD, HEAD_GROUPS, tok, HEAD_DIM), BF),
            pltpu.VMEM((PER_HEAD, tok, HEAD_GROUPS * HEAD_DIM), BF),
            pltpu.VMEM((PER_HEAD, HEAD_GROUPS, HEAD_DIM, d), BF),
            pltpu.VMEM(w_final.shape[::-1], BF),
            pltpu.VMEM((tok, d), F32),
            pltpu.VMEM((n, tok // n, 128), F32),
            pltpu.VMEM((n, tok // n, 128), F32),
            dma((3, PER_HEAD, HEAD_GROUPS)), dma((3, PER_HEAD, HEAD_GROUPS)),
            dma((2, PER_HEAD, HEAD_GROUPS, blk)), dma((2, PER_HEAD, HEAD_GROUPS, blk)),
            dma((PER_HEAD, HEAD_GROUPS)), dma((PER_HEAD, HEAD_GROUPS)),
            dma((n,)), dma((n,)),
            dma((13,)),
        ],
        compiler_params=pltpu.CompilerParams(
            collective_id=0, has_side_effects=True, vmem_limit_bytes=56 * 1024 * 1024
        ),
        name="fused",
    )(
        queries, keys, values, w_out.reshape(HEAD_GROUPS, PER_HEAD, HEAD_DIM, d),
        shift_mod.reshape(1, d), scale_mod.reshape(1, d), w_final.T,
    )
    return pl.pallas_call(
        conv_kernel,
        out_shape=jax.ShapeDtypeStruct((FRAMES, 2, 2 * ROWS, out_ch), BF),
        in_specs=[vm, vm, vm],
        out_specs=vm,
        scratch_shapes=[pltpu.VMEM((640, 2 * out_ch), BF)],
        name="conv",
    )(got, conv_weight, conv_bias.reshape(1, out_ch))


def solution(mesh):
    placed = (
        P(("groups", "seq"), None),
        P(("groups", "seq"), None),
        P(("groups", "seq"), None),
        P(),
        P("groups"),
        P("groups"),
        P(),
        P(),
        P(),
    )
    return jax.shard_map(
        shards,
        mesh=mesh,
        in_specs=placed,
        out_specs=P("groups", "seq", None, None),
        check_vma=False,
    )
```

```python
import functools
import math

import jax
import jax.numpy as jnp
from jax import lax
from jax.experimental import pallas as pl
from jax.experimental.pallas import tpu as pltpu
from jax.sharding import PartitionSpec as P

HEADS = 12
HEAD_DIM = 128
HEAD_GROUPS = 4
LATENT_CH = 16
FRAMES = 4
ROWS = 32
PER_HEAD = HEADS // HEAD_GROUPS
WIDTH = PER_HEAD * HEAD_DIM
BF = jnp.bfloat16
F32 = jnp.float32


def mm(a, b):
    return lax.dot_general(a, b, (((1,), (0,)), ((), ())), preferred_element_type=F32)


def iota(shape, dim):
    return lax.broadcasted_iota(jnp.int32, shape, dim)


def ones_where(cond):
    return jnp.where(cond, 1.0, 0.0).astype(BF)


def kernel(
    n,
    q_hbm, k_hbm, v_hbm, w_out_hbm, shift_ref, scale_ref, w_final_hbm,
    out_ref,
    q_ref, k_ref, v_ref, qb, kb, vb, m_ref, acc_ref, ob, att, w_out_v, w_final_v, proj, send_b, recv_b,
    z_send, z_recv, g_send, g_recv, o_send, o_recv, e_send, e_recv, loc,
):
    me = lax.axis_index("seq")
    blk = n // HEAD_GROUPS
    grp = me // blk
    pos = me % blk
    tok = q_hbm.shape[0]
    rows_dev = tok // n
    bits = [1 << i for i in reversed(range(blk.bit_length() - 1))]

    def cols(g, h):
        return pl.ds(pl.multiple_of(g * WIDTH + h * HEAD_DIM, 128), HEAD_DIM)

    def remote(src, dst, ssem, rsem, dev):
        return pltpu.make_async_remote_copy(
            src_ref=src, dst_ref=dst, send_sem=ssem, recv_sem=rsem,
            device_id={"seq": dev}, device_id_type=pl.DeviceIdType.MESH,
        )

    barrier = pltpu.get_barrier_semaphore()

    def greet(i, c):
        pl.semaphore_signal(
            barrier, inc=1, device_id={"seq": (me + i) % n}, device_id_type=pl.DeviceIdType.MESH
        )
        return c

    lax.fori_loop(1, n, greet, 0)

    raw = (q_hbm, k_hbm, v_hbm)
    srcs = (q_ref, k_ref, v_ref)
    staged = [pltpu.make_async_copy(raw[t], srcs[t], loc.at[13 + t]) for t in range(3)]
    bufs = (qb, kb, vb)

    def home(t, h, slot):
        return qb.at[h, slot] if t == 0 else bufs[t].at[h, slot, pos]

    own = [
        pltpu.make_async_copy(raw[t].at[:, cols(grp, h)], home(t, h, grp), loc.at[h * 3 + t])
        for h in range(PER_HEAD)
        for t in range(3)
    ]
    w_out_copies = [
        pltpu.make_async_copy(w_out_hbm.at[:, h], w_out_v.at[h], loc.at[9 + h]) for h in range(PER_HEAD)
    ]
    w_final_copy = pltpu.make_async_copy(w_final_hbm, w_final_v, loc.at[12])
    for c in staged + own + w_out_copies + [w_final_copy]:
        c.start()
    pl.semaphore_wait(barrier, n - 1)
    for c in staged:
        c.wait()

    def slot_of(j):
        return (grp + HEAD_GROUPS - j) % HEAD_GROUPS

    sent = []

    def z_start(t, h, j):
        tgt = (grp + j) % HEAD_GROUPS
        c = remote(
            srcs[t].at[:, cols(tgt, h)], home(t, h, grp),
            z_send.at[t, h, j], z_recv.at[t, h, j], tgt * blk + pos,
        )
        c.start()
        sent.append(c)

    def z_wait(t, h, j):
        dst = home(t, h, slot_of(j))
        remote(dst, dst, z_send.at[t, h, j], z_recv.at[t, h, j], slot_of(j) * blk + pos).wait_recv()

    def g_copy(t, h, j, mask, bit, src=None):
        dst = bufs[t].at[h, slot_of(j), pos ^ mask]
        return remote(
            dst if src is None else src, dst,
            g_send.at[t - 1, h, j, mask + bit], g_recv.at[t - 1, h, j, mask + bit],
            grp * blk + (pos ^ bit),
        )

    def g_wait(t, h, j, mask, bit):
        dst = bufs[t].at[h, slot_of(j), pos ^ mask]
        remote(
            dst, dst, g_send.at[t - 1, h, j, mask], g_recv.at[t - 1, h, j, mask], grp * blk + (pos ^ bit)
        ).wait_recv()

    def first(h, j):
        for t in (1, 2):
            if j:
                z_wait(t, h, j)
            for bit in bits:
                g_copy(t, h, j, 0, bit, None if j else srcs[t].at[:, cols(grp, h)]).start()

    def relay(h, j, some_bits):
        for bit in some_bits:

            def one(i, c):
                mask = bit + i * (2 * bit)
                for t in (1, 2):
                    g_wait(t, h, j, mask, bit)
                    for low in bits:
                        if low < bit:
                            g_copy(t, h, j, mask, low).start()
                return c

            lax.fori_loop(0, blk // (2 * bit), one, 0)

    for h in range(PER_HEAD):
        for j in range(1, HEAD_GROUPS):
            z_start(0, h, j)
        if h == 0:
            first(0, 0)
        for j in range(1, HEAD_GROUPS):
            for t in (1, 2):
                z_start(t, h, j)

    m_ref[...] = jnp.full(m_ref.shape, -1e30, F32)
    acc_ref[...] = jnp.zeros(acc_ref.shape, F32)
    for c in own:
        c.wait()

    queries = HEAD_GROUPS * tok
    part = min(blk, 4)
    ones = jnp.ones((part * tok, HEAD_DIM), BF)
    factor = math.log2(math.e) / math.sqrt(HEAD_DIM)

    def attend(h, slot):
        def some(i, c):
            qh = qb[h].reshape(queries, HEAD_DIM)
            kh = kb[h, slot, pl.ds(i * part, part)].reshape(part * tok, HEAD_DIM)
            vh = vb[h, slot, pl.ds(i * part, part)].reshape(part * tok, HEAD_DIM)
            s = lax.dot_general(qh, kh, (((1,), (1,)), ((), ())), preferred_element_type=F32)
            s = s * factor
            old = m_ref[h]
            new = jnp.maximum(old, jnp.max(s, axis=1, keepdims=True))
            p = jnp.exp2(s - new)
            alpha = jnp.exp2(old - new)
            acc_ref[h] = acc_ref[h] * alpha + mm(p.astype(BF), jnp.concatenate([vh, ones], axis=1))
            m_ref[h] = new
            return c

        lax.fori_loop(0, blk // part, some, 0)

    def finish(h):
        ob[h] = (acc_ref[h, :, :HEAD_DIM] / acc_ref[h, :, HEAD_DIM:]).astype(BF).reshape(HEAD_GROUPS, tok, HEAD_DIM)
        lanes = pl.ds(pl.multiple_of(grp * HEAD_DIM, 128), HEAD_DIM)
        for j in range(1, HEAD_GROUPS):
            tgt = (grp + j) % HEAD_GROUPS
            c = remote(
                ob.at[h, tgt], att.at[h, :, lanes], o_send.at[h, j], o_recv.at[h, j], tgt * blk + pos
            )
            c.start()
            sent.append(c)
        att[h, :, lanes] = ob[h, grp]

    units = [(h, j) for h in range(PER_HEAD) for j in range(HEAD_GROUPS)]
    count = len(units)
    for u in range(-2, count):
        if 0 <= u + 2 < count and u + 2 > 0:
            first(*units[u + 2])
        if 0 <= u + 1 < count:
            relay(*units[u + 1], bits[:-1])
        if u >= 0:
            h, j = units[u]
            relay(h, j, bits[-1:])
            if j == 0:
                for i in range(1, HEAD_GROUPS):
                    z_wait(0, h, i)
            attend(h, slot_of(j))
            if j == HEAD_GROUPS - 1:
                finish(h)

    for h in range(PER_HEAD):
        w_out_copies[h].wait()
        for j in range(1, HEAD_GROUPS):
            lanes = pl.ds(pl.multiple_of(slot_of(j) * HEAD_DIM, 128), HEAD_DIM)
            dst = att.at[h, :, lanes]
            remote(dst, dst, o_send.at[h, j], o_recv.at[h, j], slot_of(j) * blk + pos).wait_recv()
        term = mm(att[h], w_out_v[h].reshape(HEAD_GROUPS * HEAD_DIM, proj.shape[1]))
        proj[...] = term if h == 0 else proj[...] + term
    projected = proj[...]
    centered = projected - jnp.mean(projected, axis=1, keepdims=True)
    variance = jnp.mean(centered * centered, axis=1, keepdims=True)
    normed = (
        centered * lax.rsqrt(variance + 1e-06) * (1.0 + scale_ref[...]) + shift_ref[...]
    ).astype(BF)
    w_final_copy.wait()
    patches = lax.dot_general(
        normed, w_final_v[...], (((1,), (1,)), ((), ())), preferred_element_type=F32
    ).astype(BF)

    ch = iota((4 * LATENT_CH, 128), 0)
    lane = iota((4 * LATENT_CH, 128), 1)
    base = 4 * (lane % 16) + 2 * (lane // 64)
    xcol = (lane // 16) % 4
    row = iota((tok, tok), 0)
    col = iota((tok, tok), 1)
    w = row // rows_dev
    here = (row % rows_dev) * n + w
    picks = (
        ((col == here - 1) & (w > 0), (xcol == 0) & (ch == base + 1)),
        ((col == here) & (w == 0), (xcol == 0) & (ch == base)),
        (col == here, ((xcol == 1) & (ch == base)) | ((xcol == 2) & (ch == base + 1))),
        ((col == here + 1) & (w < n - 1), (xcol == 3) & (ch == base)),
        ((col == here) & (w == n - 1), (xcol == 3) & (ch == base + 1)),
    )
    window = None
    for rows_pick, ch_pick in picks:
        term = mm(ones_where(rows_pick), mm(patches, ones_where(ch_pick)).astype(BF))
        window = term if window is None else window + term
    send_b[...] = window.reshape(n, rows_dev, 128)

    def e_copy(i):
        dev = (me + i) % n
        return remote(send_b.at[dev], recv_b.at[me], e_send.at[i], e_recv.at[i], dev)

    def e_start(i, c):
        e_copy(i).start()
        return c

    def e_wait(i, c):
        src = (me + n - i) % n
        remote(recv_b.at[src], recv_b.at[src], e_send.at[i], e_recv.at[i], src).wait_recv()
        e_copy(i).wait_send()
        return c

    lax.fori_loop(1, n, e_start, 0)
    recv_b[me] = send_b[me]
    lax.fori_loop(1, n, e_wait, 0)
    for c in sent:
        c.wait_send()

    def drain(i, c):
        h = i // (HEAD_GROUPS * (blk - 1))
        j = (i // (blk - 1)) % HEAD_GROUPS
        mask = i % (blk - 1) + 1
        for t in (1, 2):
            ref = bufs[t].at[0, 0, 0]
            remote(
                ref, ref, g_send.at[t - 1, h, j, mask], g_recv.at[t - 1, h, j, mask], (me + 1) % n
            ).wait_send()
        return c

    lax.fori_loop(0, PER_HEAD * HEAD_GROUPS * (blk - 1), drain, 0)
    out_ref[...] = recv_b[...].reshape(out_ref.shape)


def conv_kernel(got_ref, conv_v, bias_ref, out_ref, big_w):
    out_ch = conv_v.shape[1]
    big_w[...] = jnp.zeros(big_w.shape, BF)
    for a in range(3):
        for e in range(3):
            for b in range(3):
                for s in range(2):
                    big_w[
                        (a * 3 + e) * 64 + (b + s) * 16 : (a * 3 + e) * 64 + (b + s) * 16 + 16,
                        s * out_ch : (s + 1) * out_ch,
                    ] = conv_v[(9 * a + 3 * b + e) * 16 : (9 * a + 3 * b + e) * 16 + 16, :]
    got = got_ref[...]
    turned = pltpu.roll(got, 64, 1)
    low = iota(got.shape, 1) < 64
    lo = jnp.concatenate([jnp.where(low, got, 0.0), jnp.where(low, turned, 0.0)], axis=0).astype(BF)
    hi = jnp.concatenate([jnp.where(low, 0.0, turned), jnp.where(low, 0.0, got)], axis=0).astype(BF)
    cells = FRAMES * 2 * ROWS
    orow = iota((cells, cells), 0)
    ocol = iota((cells, cells), 1)
    of = orow // (2 * ROWS)
    oy = orow % (2 * ROWS)

    def pick(idx):
        a, e = idx // 3, idx % 3
        sf = jnp.maximum(of + (a - 2), 0)
        sy = jnp.clip(oy + (e - 1), 0, 2 * ROWS - 1)
        return ones_where(ocol == (sy % 2) * (FRAMES * ROWS) + sf * ROWS + sy // 2)

    feats = []
    for pair in range(5):
        x = mm(pick(2 * pair), lo)
        if 2 * pair + 1 < 9:
            x = x + mm(pick(2 * pair + 1), hi)
        feats.append(x.astype(BF))
    feats = jnp.concatenate(feats, axis=1)
    for s in range(2):
        res = mm(feats, big_w[:, s * out_ch : (s + 1) * out_ch]) + bias_ref[...]
        res = res.astype(BF)
        for f in range(FRAMES):
            out_ref[f, s] = res[f * 2 * ROWS : (f + 1) * 2 * ROWS]

def shards(queries, keys, values, w_out, shift_mod, scale_mod, w_final, conv_weight, conv_bias):
    n = lax.axis_size("seq")
    blk = n // HEAD_GROUPS
    tok = queries.shape[0]
    d = w_out.shape[1]
    out_ch = conv_weight.shape[1]
    vm = pl.BlockSpec(memory_space=pltpu.VMEM)
    hbm = pl.BlockSpec(memory_space=pl.ANY)
    dma = pltpu.SemaphoreType.DMA
    qn = HEAD_GROUPS * tok
    got = pl.pallas_call(
        functools.partial(kernel, n),
        out_shape=jax.ShapeDtypeStruct((FRAMES * ROWS, 128), F32),
        in_specs=[hbm, hbm, hbm, hbm, vm, vm, hbm],
        out_specs=vm,
        scratch_shapes=[
            pltpu.VMEM(queries.shape, BF),
            pltpu.VMEM(keys.shape, BF),
            pltpu.VMEM(values.shape, BF),
            pltpu.VMEM((PER_HEAD, HEAD_GROUPS, tok, HEAD_DIM), BF),
            pltpu.VMEM((PER_HEAD, HEAD_GROUPS, blk, tok, HEAD_DIM), BF),
            pltpu.VMEM((PER_HEAD, HEAD_GROUPS, blk, tok, HEAD_DIM), BF),
            pltpu.VMEM((PER_HEAD, qn, 1), F32),
            pltpu.VMEM((PER_HEAD, qn, 2 * HEAD_DIM), F32),
            pltpu.VMEM((PER_HEAD, HEAD_GROUPS, tok, HEAD_DIM), BF),
            pltpu.VMEM((PER_HEAD, tok, HEAD_GROUPS * HEAD_DIM), BF),
            pltpu.VMEM((PER_HEAD, HEAD_GROUPS, HEAD_DIM, d), BF),
            pltpu.VMEM(w_final.shape[::-1], BF),
            pltpu.VMEM((tok, d), F32),
            pltpu.VMEM((n, tok // n, 128), F32),
            pltpu.VMEM((n, tok // n, 128), F32),
            dma((3, PER_HEAD, HEAD_GROUPS)), dma((3, PER_HEAD, HEAD_GROUPS)),
            dma((2, PER_HEAD, HEAD_GROUPS, blk)), dma((2, PER_HEAD, HEAD_GROUPS, blk)),
            dma((PER_HEAD, HEAD_GROUPS)), dma((PER_HEAD, HEAD_GROUPS)),
            dma((n,)), dma((n,)),
            dma((16,)),
        ],
        compiler_params=pltpu.CompilerParams(
            collective_id=0, has_side_effects=True, vmem_limit_bytes=56 * 1024 * 1024
        ),
        name="fused",
    )(
        queries, keys, values, w_out.reshape(HEAD_GROUPS, PER_HEAD, HEAD_DIM, d),
        shift_mod.reshape(1, d), scale_mod.reshape(1, d), w_final.T,
    )
    return pl.pallas_call(
        conv_kernel,
        out_shape=jax.ShapeDtypeStruct((FRAMES, 2, 2 * ROWS, out_ch), BF),
        in_specs=[vm, vm, vm],
        out_specs=vm,
        scratch_shapes=[pltpu.VMEM((640, 2 * out_ch), BF)],
        name="conv",
    )(got, conv_weight, conv_bias.reshape(1, out_ch))


def solution(mesh):
    placed = (
        P(("groups", "seq"), None),
        P(("groups", "seq"), None),
        P(("groups", "seq"), None),
        P(),
        P("groups"),
        P("groups"),
        P(),
        P(),
        P(),
    )
    return jax.shard_map(
        shards,
        mesh=mesh,
        in_specs=placed,
        out_specs=P("groups", "seq", None, None),
        check_vma=False,
    )
```

```python
import functools
import math

import jax
import jax.numpy as jnp
from jax import lax
from jax.experimental import pallas as pl
from jax.experimental.pallas import tpu as pltpu
from jax.sharding import PartitionSpec as P

HEADS = 12
HEAD_DIM = 128
HEAD_GROUPS = 4
LATENT_CH = 16
FRAMES = 4
ROWS = 32
PER_HEAD = HEADS // HEAD_GROUPS
WIDTH = PER_HEAD * HEAD_DIM
BF = jnp.bfloat16
F32 = jnp.float32


def mm(a, b):
    return lax.dot_general(a, b, (((1,), (0,)), ((), ())), preferred_element_type=F32)


def iota(shape, dim):
    return lax.broadcasted_iota(jnp.int32, shape, dim)


def ones_where(cond):
    return jnp.where(cond, 1.0, 0.0).astype(BF)


def kernel(
    n,
    q_hbm, k_hbm, v_hbm, w_out_hbm, shift_ref, scale_ref, w_final_hbm,
    out_ref,
    q_ref, k_ref, v_ref, qb, kb, vb, m_ref, acc_ref, ob, att, w_out_v, w_final_v, proj, send_b, recv_b,
    z_send, z_recv, g_send, g_recv, o_send, o_recv, e_send, e_recv, loc,
):
    me = lax.axis_index("seq")
    blk = n // HEAD_GROUPS
    grp = me // blk
    pos = me % blk
    tok = q_hbm.shape[0]
    rows_dev = tok // n
    bits = [1 << i for i in reversed(range(blk.bit_length() - 1))]

    def cols(g, h):
        return pl.ds(pl.multiple_of(g * WIDTH + h * HEAD_DIM, 128), HEAD_DIM)

    def remote(src, dst, ssem, rsem, dev):
        return pltpu.make_async_remote_copy(
            src_ref=src, dst_ref=dst, send_sem=ssem, recv_sem=rsem,
            device_id={"seq": dev}, device_id_type=pl.DeviceIdType.MESH,
        )

    barrier = pltpu.get_barrier_semaphore()

    def greet(i, c):
        pl.semaphore_signal(
            barrier, inc=1, device_id={"seq": (me + i) % n}, device_id_type=pl.DeviceIdType.MESH
        )
        return c

    lax.fori_loop(1, n, greet, 0)

    raw = (q_hbm, k_hbm, v_hbm)
    srcs = (q_ref, k_ref, v_ref)
    staged = [pltpu.make_async_copy(raw[t], srcs[t], loc.at[13 + t]) for t in range(3)]
    bufs = (qb, kb, vb)

    def home(t, h, slot):
        return qb.at[h, slot] if t == 0 else bufs[t].at[h, slot, pos]

    own = [
        pltpu.make_async_copy(raw[t].at[:, cols(grp, h)], home(t, h, grp), loc.at[h * 3 + t])
        for h in range(PER_HEAD)
        for t in range(3)
    ]
    w_out_copies = [
        pltpu.make_async_copy(w_out_hbm.at[:, h], w_out_v.at[h], loc.at[9 + h]) for h in range(PER_HEAD)
    ]
    w_final_copy = pltpu.make_async_copy(w_final_hbm, w_final_v, loc.at[12])
    for c in staged + own + w_out_copies + [w_final_copy]:
        c.start()
    pl.semaphore_wait(barrier, n - 1)
    for c in staged:
        c.wait()

    def slot_of(j):
        return (grp + HEAD_GROUPS - j) % HEAD_GROUPS

    sent = []

    def z_start(t, h, j):
        tgt = (grp + j) % HEAD_GROUPS
        c = remote(
            srcs[t].at[:, cols(tgt, h)], home(t, h, grp),
            z_send.at[t, h, j], z_recv.at[t, h, j], tgt * blk + pos,
        )
        c.start()
        sent.append(c)

    def z_wait(t, h, j):
        dst = home(t, h, slot_of(j))
        remote(dst, dst, z_send.at[t, h, j], z_recv.at[t, h, j], slot_of(j) * blk + pos).wait_recv()

    def g_copy(t, h, j, mask, bit, src=None):
        dst = bufs[t].at[h, slot_of(j), pos ^ mask]
        return remote(
            dst if src is None else src, dst,
            g_send.at[t - 1, h, j, mask + bit], g_recv.at[t - 1, h, j, mask + bit],
            grp * blk + (pos ^ bit),
        )

    def g_wait(t, h, j, mask, bit):
        dst = bufs[t].at[h, slot_of(j), pos ^ mask]
        remote(
            dst, dst, g_send.at[t - 1, h, j, mask], g_recv.at[t - 1, h, j, mask], grp * blk + (pos ^ bit)
        ).wait_recv()

    def first(h, j):
        for t in (1, 2):
            if j:
                z_wait(t, h, j)
            for bit in bits:
                g_copy(t, h, j, 0, bit, None if j else srcs[t].at[:, cols(grp, h)]).start()

    def relay(h, j, some_bits):
        for bit in some_bits:

            def one(i, c):
                mask = bit + i * (2 * bit)
                for t in (1, 2):
                    g_wait(t, h, j, mask, bit)
                    for low in bits:
                        if low < bit:
                            g_copy(t, h, j, mask, low).start()
                return c

            lax.fori_loop(0, blk // (2 * bit), one, 0)

    order = (0, 2, 1, 3)
    for h in range(PER_HEAD):
        for j in order[1:]:
            z_start(0, h, j)
        if h == 0:
            first(0, 0)
        for j in order[1:]:
            for t in (1, 2):
                z_start(t, h, j)

    m_ref[...] = jnp.full(m_ref.shape, -1e30, F32)
    acc_ref[...] = jnp.zeros(acc_ref.shape, F32)
    for c in own:
        c.wait()

    queries = HEAD_GROUPS * tok
    part = min(blk, 4)
    ones = jnp.ones((part * tok, HEAD_DIM), BF)
    factor = math.log2(math.e) / math.sqrt(HEAD_DIM)

    def attend(h, slot):
        def some(i, c):
            qh = qb[h].reshape(queries, HEAD_DIM)
            kh = kb[h, slot, pl.ds(i * part, part)].reshape(part * tok, HEAD_DIM)
            vh = vb[h, slot, pl.ds(i * part, part)].reshape(part * tok, HEAD_DIM)
            s = lax.dot_general(qh, kh, (((1,), (1,)), ((), ())), preferred_element_type=F32)
            s = s * factor
            old = m_ref[h]
            new = jnp.maximum(old, jnp.max(s, axis=1, keepdims=True))
            p = jnp.exp2(s - new)
            alpha = jnp.exp2(old - new)
            acc_ref[h] = acc_ref[h] * alpha + mm(p.astype(BF), jnp.concatenate([vh, ones], axis=1))
            m_ref[h] = new
            return c

        lax.fori_loop(0, blk // part, some, 0)

    def finish(h):
        ob[h] = (acc_ref[h, :, :HEAD_DIM] / acc_ref[h, :, HEAD_DIM:]).astype(BF).reshape(HEAD_GROUPS, tok, HEAD_DIM)
        lanes = pl.ds(pl.multiple_of(grp * HEAD_DIM, 128), HEAD_DIM)
        for j in range(1, HEAD_GROUPS):
            tgt = (grp + j) % HEAD_GROUPS
            c = remote(
                ob.at[h, tgt], att.at[h, :, lanes], o_send.at[h, j], o_recv.at[h, j], tgt * blk + pos
            )
            c.start()
            sent.append(c)
        att[h, :, lanes] = ob[h, grp]

    units = [(h, j) for h in range(PER_HEAD) for j in order]
    count = len(units)
    for u in range(-2, count):
        if 0 <= u + 2 < count and u + 2 > 0:
            first(*units[u + 2])
        if 0 <= u + 1 < count:
            relay(*units[u + 1], bits[:-1])
        if u >= 0:
            h, j = units[u]
            relay(h, j, bits[-1:])
            if j == 0:
                for i in range(1, HEAD_GROUPS):
                    z_wait(0, h, i)
            attend(h, slot_of(j))
            if j == order[-1]:
                finish(h)

    for h in range(PER_HEAD):
        w_out_copies[h].wait()
        for j in range(1, HEAD_GROUPS):
            lanes = pl.ds(pl.multiple_of(slot_of(j) * HEAD_DIM, 128), HEAD_DIM)
            dst = att.at[h, :, lanes]
            remote(dst, dst, o_send.at[h, j], o_recv.at[h, j], slot_of(j) * blk + pos).wait_recv()
        term = mm(att[h], w_out_v[h].reshape(HEAD_GROUPS * HEAD_DIM, proj.shape[1]))
        proj[...] = term if h == 0 else proj[...] + term
    projected = proj[...]
    centered = projected - jnp.mean(projected, axis=1, keepdims=True)
    variance = jnp.mean(centered * centered, axis=1, keepdims=True)
    normed = (
        centered * lax.rsqrt(variance + 1e-06) * (1.0 + scale_ref[...]) + shift_ref[...]
    ).astype(BF)
    w_final_copy.wait()
    patches = lax.dot_general(
        normed, w_final_v[...], (((1,), (1,)), ((), ())), preferred_element_type=F32
    ).astype(BF)

    ch = iota((4 * LATENT_CH, 128), 0)
    lane = iota((4 * LATENT_CH, 128), 1)
    base = 4 * (lane % 16) + 2 * (lane // 64)
    xcol = (lane // 16) % 4
    row = iota((tok, tok), 0)
    col = iota((tok, tok), 1)
    w = row // rows_dev
    here = (row % rows_dev) * n + w
    picks = (
        ((col == here - 1) & (w > 0), (xcol == 0) & (ch == base + 1)),
        ((col == here) & (w == 0), (xcol == 0) & (ch == base)),
        (col == here, ((xcol == 1) & (ch == base)) | ((xcol == 2) & (ch == base + 1))),
        ((col == here + 1) & (w < n - 1), (xcol == 3) & (ch == base)),
        ((col == here) & (w == n - 1), (xcol == 3) & (ch == base + 1)),
    )
    window = None
    for rows_pick, ch_pick in picks:
        term = mm(ones_where(rows_pick), mm(patches, ones_where(ch_pick)).astype(BF))
        window = term if window is None else window + term
    send_b[...] = window.reshape(n, rows_dev, 128)

    def e_copy(i):
        dev = (me + i) % n
        return remote(send_b.at[dev], recv_b.at[me], e_send.at[i], e_recv.at[i], dev)

    def e_start(i, c):
        e_copy(i).start()
        return c

    def e_wait(i, c):
        src = (me + n - i) % n
        remote(recv_b.at[src], recv_b.at[src], e_send.at[i], e_recv.at[i], src).wait_recv()
        e_copy(i).wait_send()
        return c

    lax.fori_loop(1, n, e_start, 0)
    recv_b[me] = send_b[me]
    lax.fori_loop(1, n, e_wait, 0)
    for c in sent:
        c.wait_send()

    def drain(i, c):
        h = i // (HEAD_GROUPS * (blk - 1))
        j = (i // (blk - 1)) % HEAD_GROUPS
        mask = i % (blk - 1) + 1
        for t in (1, 2):
            ref = bufs[t].at[0, 0, 0]
            remote(
                ref, ref, g_send.at[t - 1, h, j, mask], g_recv.at[t - 1, h, j, mask], (me + 1) % n
            ).wait_send()
        return c

    lax.fori_loop(0, PER_HEAD * HEAD_GROUPS * (blk - 1), drain, 0)
    out_ref[...] = recv_b[...].reshape(out_ref.shape)


def conv_kernel(got_ref, conv_v, bias_ref, out_ref, big_w):
    out_ch = conv_v.shape[1]
    big_w[...] = jnp.zeros(big_w.shape, BF)
    for a in range(3):
        for e in range(3):
            for b in range(3):
                for s in range(2):
                    big_w[
                        (a * 3 + e) * 64 + (b + s) * 16 : (a * 3 + e) * 64 + (b + s) * 16 + 16,
                        s * out_ch : (s + 1) * out_ch,
                    ] = conv_v[(9 * a + 3 * b + e) * 16 : (9 * a + 3 * b + e) * 16 + 16, :]
    got = got_ref[...]
    turned = pltpu.roll(got, 64, 1)
    low = iota(got.shape, 1) < 64
    lo = jnp.concatenate([jnp.where(low, got, 0.0), jnp.where(low, turned, 0.0)], axis=0).astype(BF)
    hi = jnp.concatenate([jnp.where(low, 0.0, turned), jnp.where(low, 0.0, got)], axis=0).astype(BF)
    cells = FRAMES * 2 * ROWS
    orow = iota((cells, cells), 0)
    ocol = iota((cells, cells), 1)
    of = orow // (2 * ROWS)
    oy = orow % (2 * ROWS)

    def pick(idx):
        a, e = idx // 3, idx % 3
        sf = jnp.maximum(of + (a - 2), 0)
        sy = jnp.clip(oy + (e - 1), 0, 2 * ROWS - 1)
        return ones_where(ocol == (sy % 2) * (FRAMES * ROWS) + sf * ROWS + sy // 2)

    feats = []
    for pair in range(5):
        x = mm(pick(2 * pair), lo)
        if 2 * pair + 1 < 9:
            x = x + mm(pick(2 * pair + 1), hi)
        feats.append(x.astype(BF))
    feats = jnp.concatenate(feats, axis=1)
    for s in range(2):
        res = mm(feats, big_w[:, s * out_ch : (s + 1) * out_ch]) + bias_ref[...]
        res = res.astype(BF)
        for f in range(FRAMES):
            out_ref[f, s] = res[f * 2 * ROWS : (f + 1) * 2 * ROWS]

def shards(queries, keys, values, w_out, shift_mod, scale_mod, w_final, conv_weight, conv_bias):
    n = lax.axis_size("seq")
    blk = n // HEAD_GROUPS
    tok = queries.shape[0]
    d = w_out.shape[1]
    out_ch = conv_weight.shape[1]
    vm = pl.BlockSpec(memory_space=pltpu.VMEM)
    hbm = pl.BlockSpec(memory_space=pl.ANY)
    dma = pltpu.SemaphoreType.DMA
    qn = HEAD_GROUPS * tok
    got = pl.pallas_call(
        functools.partial(kernel, n),
        out_shape=jax.ShapeDtypeStruct((FRAMES * ROWS, 128), F32),
        in_specs=[hbm, hbm, hbm, hbm, vm, vm, hbm],
        out_specs=vm,
        scratch_shapes=[
            pltpu.VMEM(queries.shape, BF),
            pltpu.VMEM(keys.shape, BF),
            pltpu.VMEM(values.shape, BF),
            pltpu.VMEM((PER_HEAD, HEAD_GROUPS, tok, HEAD_DIM), BF),
            pltpu.VMEM((PER_HEAD, HEAD_GROUPS, blk, tok, HEAD_DIM), BF),
            pltpu.VMEM((PER_HEAD, HEAD_GROUPS, blk, tok, HEAD_DIM), BF),
            pltpu.VMEM((PER_HEAD, qn, 1), F32),
            pltpu.VMEM((PER_HEAD, qn, 2 * HEAD_DIM), F32),
            pltpu.VMEM((PER_HEAD, HEAD_GROUPS, tok, HEAD_DIM), BF),
            pltpu.VMEM((PER_HEAD, tok, HEAD_GROUPS * HEAD_DIM), BF),
            pltpu.VMEM((PER_HEAD, HEAD_GROUPS, HEAD_DIM, d), BF),
            pltpu.VMEM(w_final.shape[::-1], BF),
            pltpu.VMEM((tok, d), F32),
            pltpu.VMEM((n, tok // n, 128), F32),
            pltpu.VMEM((n, tok // n, 128), F32),
            dma((3, PER_HEAD, HEAD_GROUPS)), dma((3, PER_HEAD, HEAD_GROUPS)),
            dma((2, PER_HEAD, HEAD_GROUPS, blk)), dma((2, PER_HEAD, HEAD_GROUPS, blk)),
            dma((PER_HEAD, HEAD_GROUPS)), dma((PER_HEAD, HEAD_GROUPS)),
            dma((n,)), dma((n,)),
            dma((16,)),
        ],
        compiler_params=pltpu.CompilerParams(
            collective_id=0, has_side_effects=True, vmem_limit_bytes=56 * 1024 * 1024
        ),
        name="fused",
    )(
        queries, keys, values, w_out.reshape(HEAD_GROUPS, PER_HEAD, HEAD_DIM, d),
        shift_mod.reshape(1, d), scale_mod.reshape(1, d), w_final.T,
    )
    return pl.pallas_call(
        conv_kernel,
        out_shape=jax.ShapeDtypeStruct((FRAMES, 2, 2 * ROWS, out_ch), BF),
        in_specs=[vm, vm, vm],
        out_specs=vm,
        scratch_shapes=[pltpu.VMEM((640, 2 * out_ch), BF)],
        name="conv",
    )(got, conv_weight, conv_bias.reshape(1, out_ch))


def solution(mesh):
    placed = (
        P(("groups", "seq"), None),
        P(("groups", "seq"), None),
        P(("groups", "seq"), None),
        P(),
        P("groups"),
        P("groups"),
        P(),
        P(),
        P(),
    )
    return jax.shard_map(
        shards,
        mesh=mesh,
        in_specs=placed,
        out_specs=P("groups", "seq", None, None),
        check_vma=False,
    )
```
